512 devices in a mesh: dp: 8 (over z_lo, core), seq: 64 (over y, z_hi, x).
Axes of the slice: x: 4, y: 4, z: 16 (z_hi: 4, z_lo: 4; z = z_hi * 4 + z_lo), core: 2. Of those that a mesh axis runs over, the one named last changes fastest.
Arguments:
- inputs: bfloat16 [8, 32768, 768], P('dp', 'seq'), may hold values from -6 to 6
- cotangent: bfloat16 [8, 32768, 768], P('dp', 'seq'), may hold values from -1.5 to 1.5
- factor_one: bfloat16 [64, 512, 512], P('seq'), may hold values from -0.25 to 0.25
- factor_two: bfloat16 [512, 64, 64], P('seq'), may hold values from -0.75 to 0.75
- up_weight: bfloat16 [2, 384, 1536], P(None, None, 'dp'), may hold values from -0.3125 to 0.3125
- down_weight: bfloat16 [2, 1536, 384], P(None, 'dp'), may hold values from -0.15625 to 0.15625
Outputs:
- outputs: bfloat16 [8, 32768, 768], P('dp', 'seq')
- grad_inputs: bfloat16 [8, 32768, 768], P('dp', 'seq')
- grad_factor_one: float32 [64, 512, 512], P('seq', 'dp')
- grad_factor_two: float32 [512, 64, 64], P('seq', 'dp')
The draws below stay inside these ranges and needn't reach their ends.
All inputs are finite; a program needn't handle non-finite values.
Results may differ from the reference program's by a relative error of at most 0.0066.
Values may be sent and summed in bfloat16 or wider, within the bound.
No kernel may reach another device: no remote copies, remote signals or barrier semaphores. Data moves between devices by JAX's collectives and lax.ppermute only.
A program may use at most 64 MiB of HBM per device.

```python
import jax
import jax.numpy as jnp
from jax import lax

BLOCK = 512
GROUP_CH = 384
GROUPS = 2
GROUP_HID = 1536
BLOCKS = 64
CHANNELS = 768
SEQLEN = 32768
N_DP = 8


def shard_levels(own_key, dims, split, low, largest):
    gain, own = 1.0, jax.random.fold_in(own_key, 6)
    for position, parts in split:
        steps = jnp.exp(jax.random.uniform(jax.random.fold_in(own, position), (parts,), jnp.float32, low / len(split), largest / len(split)))
        gain = gain * jnp.repeat(steps, dims[position] // parts).reshape([-1 if axis == position else 1 for axis in range(len(dims))])
    return gain


def centred(own_key, shape, deviation, most, cuts=(), kind=jnp.bfloat16):
    loudness = shard_levels(own_key, shape, cuts, -0.22, 0.18) if cuts else 1.0
    array = jax.random.normal(own_key, shape, jnp.float32) * deviation * loudness
    return jnp.minimum(jnp.maximum(array, -most), most).astype(kind)


def setup_inputs(seed: int = 0) -> dict:
    arg_keys = jax.random.split(jax.random.key(seed), 7)
    return {
        "inputs": centred(arg_keys[0], (N_DP, SEQLEN, CHANNELS), 1.0, 6.0, ((0, 8), (1, 64))),
        "cotangent": centred(arg_keys[1], (N_DP, SEQLEN, CHANNELS), 0.25, 1.5, ((0, 8), (1, 64))),
        "factor_one": centred(arg_keys[2], (BLOCKS, BLOCK, BLOCK), BLOCK ** -0.5, 0.25, ((0, 64),)),
        "factor_two": centred(arg_keys[3], (BLOCK, BLOCKS, BLOCKS), BLOCKS ** -0.5, 0.75, ((0, 64),)),
        "up_weight": centred(arg_keys[4], (GROUPS, GROUP_CH, GROUP_HID), GROUP_CH ** -0.5, 0.3125, ((2, 8),)),
        "down_weight": centred(arg_keys[5], (GROUPS, GROUP_HID, GROUP_CH), GROUP_HID ** -0.5, 0.15625, ((1, 8),)),
    }


def reference(inputs, cotangent, factor_one, factor_two, up_weight, down_weight):
    first = factor_one.astype(jnp.float32)
    second = factor_two.astype(jnp.float32)
    up_full = up_weight.astype(jnp.float32)
    down_full = down_weight.astype(jnp.float32)

    def one_sequence(carry, pair):
        seq_in, seq_cot = pair
        blocked = seq_in.reshape(BLOCKS, BLOCK, CHANNELS).astype(jnp.float32)
        mixed_one = jnp.einsum('apb,abc->apc', first, blocked).astype(jnp.bfloat16)
        cols_one = mixed_one.astype(jnp.float32).transpose(1, 0, 2)
        mixed_pq = jnp.einsum('pqa,pac->pqc', second, cols_one).astype(jnp.bfloat16)
        mixed_two = mixed_pq.astype(jnp.float32).transpose(1, 0, 2).reshape(SEQLEN, CHANNELS)
        input_f = seq_in.astype(jnp.float32)
        silu_vals, silu_back = jax.vjp(jax.nn.silu, input_f)
        gated = (mixed_two * silu_vals).astype(jnp.bfloat16)
        gated_f = gated.astype(jnp.float32).reshape(SEQLEN, GROUPS, GROUP_CH)
        pre = jnp.einsum('tnc,nch->tnh', gated_f, up_full)
        hidden_act, gelu_back = jax.vjp(jax.nn.gelu, pre)
        hidden = hidden_act.astype(jnp.bfloat16).astype(jnp.float32)
        result = gated_f + jnp.einsum('tnh,nhc->tnc', hidden, down_full)
        result = result.reshape(SEQLEN, CHANNELS).astype(jnp.bfloat16)
        cot_f = seq_cot.astype(jnp.float32).reshape(SEQLEN, GROUPS, GROUP_CH)
        grad_hidden = jnp.einsum('tnc,nhc->tnh', cot_f, down_full)
        grad_pre = gelu_back(grad_hidden)[0].astype(jnp.bfloat16).astype(jnp.float32)
        grad_gated = cot_f + jnp.einsum('tnh,nch->tnc', grad_pre, up_full)
        grad_gated = grad_gated.reshape(SEQLEN, CHANNELS)
        grad_two = (grad_gated * silu_vals).astype(jnp.bfloat16)
        grad_gate_in = silu_back(grad_gated * mixed_two)[0]
        grad_cols = grad_two.astype(jnp.float32).reshape(BLOCKS, BLOCK, CHANNELS).transpose(1, 0, 2)
        term_two = jnp.einsum('pqc,pac->pqa', grad_cols, cols_one)
        grad_one_pa = jnp.einsum('pqa,pqc->pac', second, grad_cols).astype(jnp.bfloat16)
        grad_one = grad_one_pa.astype(jnp.float32).transpose(1, 0, 2)
        term_one = jnp.einsum('apc,abc->apb', grad_one, blocked)
        grad_in = grad_gate_in.reshape(BLOCKS, BLOCK, CHANNELS) + jnp.einsum('apb,apc->abc', first, grad_one)
        grad_in = grad_in.reshape(SEQLEN, CHANNELS).astype(jnp.bfloat16)
        return ((carry[0] + term_one, carry[1] + term_two), (result, grad_in))
    start = (jnp.zeros((BLOCKS, BLOCK, BLOCK), jnp.float32), jnp.zeros((BLOCK, BLOCKS, BLOCKS), jnp.float32))
    sums, stacked = lax.scan(one_sequence, start, (inputs, cotangent))
    return (stacked[0], stacked[1], sums[0], sums[1])
```

```python
import jax
import jax.numpy as jnp
from jax import lax
from jax.sharding import Mesh
from jax.sharding import PartitionSpec as P

F32 = jnp.float32
BF16 = jnp.bfloat16
SIDE = 4
CORES = 2
TO = ("x", "hi", "y")
WEIGHT_SLICES = 8


def nt(a, b):
    return lax.dot_general(a, b, (((1,), (1,)), ((), ())), preferred_element_type=F32)


def nn(a, b):
    return lax.dot_general(a, b, (((1,), (0,)), ((), ())), preferred_element_type=F32)


def tn(a, b):
    return lax.dot_general(a, b, (((0,), (0,)), ((), ())), preferred_element_type=F32)


def swap(x, axis=0):
    shape = x.shape
    rest = shape[axis] // SIDE**3
    x = x.reshape(shape[:axis] + (SIDE, SIDE, SIDE, rest) + shape[axis + 1 :])
    return jnp.swapaxes(x, axis, axis + 2).reshape(shape)


def exchange(x, blocks):
    out = lax.all_to_all(
        x.reshape(blocks, x.shape[0] // blocks, x.shape[1]), TO, split_axis=0, concat_axis=0, tiled=True
    )
    return out.reshape(x.shape)


def shift(x, axis, step):
    return lax.ppermute(x, axis, [(i, (i + step) % SIDE) for i in range(SIDE)])


def gather_weights(up_weight, down_weight):
    groups, group_ch, own_hid = up_weight.shape
    rows = own_hid // WEIGHT_SLICES
    own = jnp.stack([jnp.swapaxes(up_weight, 1, 2), down_weight], axis=1)
    place = lax.axis_index("y") * 2 + lax.rem(lax.axis_index("x"), 2)
    piece = lax.dynamic_slice_in_dim(own, place * rows, rows, axis=2)
    column = jnp.concatenate([piece] + [shift(piece, "lo", k) for k in (1, 2, 3)], axis=2)
    pair = jnp.concatenate([column, lax.ppermute(column, "x", [(i, i ^ 1) for i in range(SIDE)])], axis=2)
    return pair


def spread_weights(pair):
    plane = jnp.concatenate([pair] + [shift(pair, "y", k) for k in (1, 2, 3)], axis=2)
    other = lax.ppermute(plane, "core", [(0, 1), (1, 0)])
    return plane, other


def shards(inputs, cotangent, factor_one, factor_two, up_weight, down_weight):
    groups, group_ch, _ = up_weight.shape
    block = factor_one.shape[1]
    own_p, blocks, _ = factor_two.shape
    n_dp = SIDE * CORES
    x_nat = inputs[0]
    one = swap(factor_one[0])

    cols_one = exchange(nn(one, x_nat).astype(BF16), blocks)

    eye = jnp.eye(own_p, dtype=BF16)
    two = jnp.transpose(swap(swap(factor_two, 1), 2), (1, 0, 2))
    two = (two[:, :, :, None] * eye[None, :, None, :]).reshape(block, block)
    pair = gather_weights(up_weight, down_weight)
    x_all, cot_all = swap(x_nat), swap(cotangent[0])
    cols_one, pair, two, x_all, cot_all = lax.optimization_barrier((cols_one, pair, two, x_all, cot_all))

    weights = spread_weights(pair)
    mixed = exchange(nn(two, cols_one).astype(BF16), blocks)

    def cols(a, g):
        return lax.slice_in_dim(a, g * group_ch, (g + 1) * group_ch, axis=1)

    mixed_f = mixed.astype(F32)
    silu_vals, silu_back = jax.vjp(jax.nn.silu, x_all.astype(F32))
    gated = (mixed_f * silu_vals).astype(BF16)
    results, grads = [], []
    for g in range(groups):
        cot = cols(cot_all, g)
        result, grad_gated = cols(gated, g).astype(F32), cot.astype(F32)
        for w in weights:
            up, down = w[g, 0], w[g, 1]
            hidden, gelu_back = jax.vjp(jax.nn.gelu, nt(cols(gated, g), up))
            result = result + nn(hidden.astype(BF16), down)
            grad_pre = gelu_back(nt(cot, down))[0].astype(BF16)
            grad_gated = grad_gated + nn(grad_pre, up)
        results.append(result.astype(BF16))
        grads.append(grad_gated)
    grad_gated = jnp.concatenate(grads, axis=1)
    grad_cols = exchange((grad_gated * silu_vals).astype(BF16), blocks)
    outputs = swap(jnp.concatenate(results, axis=1))[None]
    gate_in = swap(silu_back(grad_gated * mixed_f)[0])
    grad_cols, outputs, gate_in = lax.optimization_barrier((grad_cols, outputs, gate_in))

    grad_one = exchange(tn(two, grad_cols).astype(BF16), blocks)

    same = jnp.tile(jnp.eye(own_p, dtype=F32), (blocks, blocks))
    pick = swap(jnp.repeat(jnp.eye(blocks, dtype=BF16), own_p, axis=0))
    term_two = nn((nt(grad_cols, cols_one) * same).astype(BF16), pick).astype(BF16)
    term_two = swap(term_two.reshape(blocks, own_p * blocks)).reshape(n_dp, -1, block)
    grad_one, term_two = lax.optimization_barrier((grad_one, term_two))
    term_one = swap(nt(grad_one, x_nat).astype(BF16)).reshape(n_dp, block // n_dp, block)
    summed = lax.all_to_all(
        jnp.concatenate([term_one, term_two], axis=1), ("lo", "core"), split_axis=0, concat_axis=0, tiled=True
    )
    summed = jnp.sum(summed.astype(F32), axis=0)
    grad_first = summed[: block // n_dp][None]
    grad_second = jnp.transpose(summed[block // n_dp :].reshape(blocks // n_dp, own_p, blocks), (1, 0, 2))

    grad_inputs = (gate_in + tn(one, grad_one)).astype(BF16)[None]
    return outputs, grad_inputs, grad_first, grad_second


def solution(mesh):
    grid = Mesh(mesh.devices.reshape(SIDE, CORES, SIDE, SIDE, SIDE), ("lo", "core", "y", "hi", "x"))
    dp, seq = ("lo", "core"), ("y", "hi", "x")
    in_specs = (P(dp, seq, None), P(dp, seq, None), P(seq, None, None), P(seq, None, None), P(None, None, dp), P(None, dp, None))
    out_specs = (P(dp, seq, None), P(dp, seq, None), P(seq, dp, None), P(seq, dp, None))
    return jax.shard_map(shards, mesh=grid, in_specs=in_specs, out_specs=out_specs, check_vma=False)
```

```python
import functools

import jax
import jax.numpy as jnp
from jax import lax
from jax.experimental import pallas as pl
from jax.experimental.pallas import tpu as pltpu
from jax.sharding import Mesh
from jax.sharding import PartitionSpec as P


F32 = jnp.float32
BF16 = jnp.bfloat16
SIDE = 4
CORES = 2
RING = SIDE * SIDE
TO = ("x", "hi", "y")
WEIGHT_SLICES = 8
C0 = 0.7978845608028654
C1 = 0.044715


def nt(a, b):
    return lax.dot_general(a, b, (((1,), (1,)), ((), ())), preferred_element_type=F32)


def nn(a, b):
    return lax.dot_general(a, b, (((1,), (0,)), ((), ())), preferred_element_type=F32)


def tn(a, b):
    return lax.dot_general(a, b, (((0,), (0,)), ((), ())), preferred_element_type=F32)


def swap(x, axis=0):
    shape = x.shape
    rest = shape[axis] // SIDE**3
    x = x.reshape(shape[:axis] + (SIDE, SIDE, SIDE, rest) + shape[axis + 1 :])
    return jnp.swapaxes(x, axis, axis + 2).reshape(shape)


def exchange(x, blocks):
    out = lax.all_to_all(
        x.reshape(blocks, x.shape[0] // blocks, x.shape[1]), TO, split_axis=0, concat_axis=0, tiled=True
    )
    return out.reshape(x.shape)


def along_z(x, step):
    at = [(z % SIDE) * SIDE + z // SIDE for z in range(RING)]
    return lax.ppermute(x, ("lo", "hi"), [(at[z], at[(z + step) % RING]) for z in range(RING)])


def shift(x, axis, step):
    return lax.ppermute(x, axis, [(i, (i + step) % SIDE) for i in range(SIDE)])


def gate(m_ref, x_ref):
    x = x_ref[...].astype(F32)
    return (m_ref[...].astype(F32) * (x * jax.nn.sigmoid(x))).astype(BF16)


def grads_kernel(m_ref, x_ref, c_ref, own_ref, other_ref, two_ref, grad_ref, gated, total):
    half = pl.program_id(1)

    @pl.when(half == 0)
    def _():
        gated[...] = gate(m_ref, x_ref)
        total[...] = c_ref[...].astype(F32)

    def add(w_ref):
        up, down = w_ref[0, 0], w_ref[0, 1]
        pre = nt(gated[...], up)
        back = nt(c_ref[...], down)
        square = pre * pre
        t = jnp.tanh(pre * (C0 + (C0 * C1) * square))
        slope = 0.5 + 0.5 * t + (0.5 * pre) * (1.0 - t * t) * (C0 + (3.0 * C0 * C1) * square)
        total[...] += nn((back * slope).astype(BF16), up)

    @pl.when(half == 0)
    def _():
        add(own_ref)

    @pl.when(half == 1)
    def _():
        add(other_ref)
        x = x_ref[...].astype(F32)
        grad_ref[...] = total[...]
        two_ref[...] = (total[...] * (x * jax.nn.sigmoid(x))).astype(BF16)


def outputs_kernel(rows, m_ref, x_ref, own_ref, other_ref, out_ref, gated, total):
    half = pl.program_id(1)

    @pl.when(half == 0)
    def _():
        gated[...] = gate(m_ref, x_ref)
        total[...] = gated[...].astype(F32)

    def add(w_ref):
        up, down = w_ref[0, 0], w_ref[0, 1]
        for at in range(0, gated.shape[0], rows):
            part = pl.ds(at, rows)
            pre = nt(gated[part, :], up)
            t = jnp.tanh(pre * (C0 + (C0 * C1) * (pre * pre)))
            total[part, :] += nn((pre * (0.5 + 0.5 * t)).astype(BF16), down)

    @pl.when(half == 0)
    def _():
        add(own_ref)

    @pl.when(half == 1)
    def _():
        add(other_ref)
        out_ref[...] = total[...].astype(BF16)


def mlp_call(kernel, arrays, weights, out_types, dots):
    tokens, channels = arrays[0].shape
    groups, _, hid, group_ch = weights[0].shape
    cols = pl.BlockSpec((tokens, group_ch), lambda g, h: (0, g))
    whole = pl.BlockSpec((1, 2, hid, group_ch), lambda g, h: (g, 0, 0, 0))
    units = len(weights) * hid
    return pl.pallas_call(
        kernel,
        grid=(groups, len(weights)),
        in_specs=[cols] * len(arrays) + [whole] * len(weights),
        out_specs=[cols] * len(out_types),
        out_shape=[jax.ShapeDtypeStruct((tokens, channels), t) for t in out_types],
        scratch_shapes=[pltpu.VMEM((tokens, group_ch), BF16), pltpu.VMEM((tokens, group_ch), F32)],
        cost_estimate=pl.CostEstimate(
            flops=2 * dots * tokens * channels * units,
            transcendentals=tokens * units * groups,
            bytes_accessed=2 * len(arrays) * tokens * channels + 4 * channels * units,
        ),
    )(*arrays, *weights)


def weight_column(up_weight, down_weight):
    own_hid = up_weight.shape[2]
    rows = own_hid // WEIGHT_SLICES
    own = jnp.stack([jnp.swapaxes(up_weight, 1, 2), down_weight], axis=1)
    place = lax.axis_index("y") * 2 + lax.rem(lax.axis_index("x"), 2)
    piece = lax.dynamic_slice_in_dim(own, place * rows, rows, axis=2)
    column = [along_z(piece, step) for step in (1, -1, 2)]
    return own, jnp.concatenate(column, axis=2)


def weight_pair(column):
    other = lax.ppermute(column, "x", [(i, i ^ 1) for i in range(SIDE)])
    return jnp.concatenate([column, other], axis=2)


def weight_halves(own, pair):
    others = [shift(pair, "y", k) for k in (1, 2, 3)]
    half = jnp.concatenate([own, pair] + others, axis=2)
    return half, lax.ppermute(half, "core", [(0, 1), (1, 0)])


def layer(inputs, cotangent, factor_one, factor_two, up_weight, down_weight):
    block = factor_one.shape[1]
    own_p, blocks, _ = factor_two.shape
    n_dp = SIDE * CORES
    x_nat = inputs[0]

    own, column = weight_column(up_weight, down_weight)
    one = swap(factor_one[0])
    mixed_one = nn(one, x_nat).astype(BF16)
    mixed_one, column = lax.optimization_barrier((mixed_one, column))
    cols_one = exchange(mixed_one, blocks)

    at = lax.broadcasted_iota(jnp.int32, (blocks, block), 1) // own_p
    at = lax.rem(at, SIDE) * SIDE**2 + lax.rem(at // SIDE, SIDE) * SIDE + at // SIDE**2
    pick = (at == lax.broadcasted_iota(jnp.int32, (blocks, block), 0)).astype(BF16)

    def diagonal(full):
        row = lax.broadcasted_iota(jnp.int32, (block, block), 0)
        col = lax.broadcasted_iota(jnp.int32, (block, block), 1)
        return jnp.where(lax.rem(row, own_p) == lax.rem(col, own_p), full, 0.0).astype(BF16)

    by_q = swap(jnp.transpose(factor_two, (1, 0, 2))).reshape(block, blocks)
    two = diagonal(nn(by_q, pick))
    pair = weight_pair(column)
    x_all, cot_all = swap(x_nat), swap(cotangent[0])
    cols_one, _, two, x_all, cot_all = lax.optimization_barrier((cols_one, pair, two, x_all, cot_all))

    weights = weight_halves(own, pair)
    mixed_two = nn(two, cols_one).astype(BF16)
    mixed = exchange(mixed_two, blocks)

    grad_two, grad_gated = mlp_call(grads_kernel, (mixed, x_all, cot_all), weights, (BF16, F32), 3)
    grad_cols = exchange(grad_two, blocks)

    (outputs,) = mlp_call(functools.partial(outputs_kernel, 256), (mixed, x_all), weights, (BF16,), 2)
    outputs = swap(outputs)[None]
    gate_in = swap(jax.vjp(jax.nn.silu, x_all.astype(F32))[1](grad_gated * mixed.astype(F32))[0])
    grad_cols, outputs, gate_in = lax.optimization_barrier((grad_cols, outputs, gate_in))

    grad_one = exchange(tn(two, grad_cols).astype(BF16), blocks)

    term_two = nt(diagonal(nt(grad_cols, cols_one)), pick).astype(BF16)
    term_two = swap(term_two.reshape(blocks, own_p * blocks)).reshape(n_dp, -1, block)
    grad_one, term_two = lax.optimization_barrier((grad_one, term_two))

    term_one = swap(nt(grad_one, x_nat).astype(BF16)).reshape(n_dp, block // n_dp, block)
    summed = lax.all_to_all(
        jnp.concatenate([term_one, term_two], axis=1), ("lo", "core"), split_axis=0, concat_axis=0, tiled=True
    )
    summed = jnp.sum(summed.astype(F32), axis=0)
    grad_first = summed[: block // n_dp][None]
    grad_second = jnp.transpose(summed[block // n_dp :].reshape(blocks // n_dp, own_p, blocks), (1, 0, 2))

    grad_inputs = (gate_in + tn(one, grad_one)).astype(BF16)[None]
    return outputs, grad_inputs, grad_first, grad_second


def solution(mesh):
    grid = Mesh(mesh.devices.reshape(SIDE, CORES, SIDE, SIDE, SIDE), ("lo", "core", "y", "hi", "x"))
    dp, seq = ("lo", "core"), ("y", "hi", "x")
    in_specs = (P(dp, seq, None), P(dp, seq, None), P(seq, None, None), P(seq, None, None), P(None, None, dp), P(None, dp, None))
    out_specs = (P(dp, seq, None), P(dp, seq, None), P(seq, dp, None), P(seq, dp, None))
    return jax.shard_map(layer, mesh=grid, in_specs=in_specs, out_specs=out_specs, check_vma=False)
```

```python
import functools

import jax
import jax.numpy as jnp
from jax import lax
from jax.experimental import pallas as pl
from jax.experimental.pallas import tpu as pltpu
from jax.sharding import Mesh
from jax.sharding import PartitionSpec as P


F32 = jnp.float32
BF16 = jnp.bfloat16
SIDE = 4
CORES = 2
TO = ("x", "hi", "y")
WEIGHT_SLICES = 8
C0 = 0.7978845608028654
C1 = 0.044715


def nt(a, b):
    return lax.dot_general(a, b, (((1,), (1,)), ((), ())), preferred_element_type=F32)


def nn(a, b):
    return lax.dot_general(a, b, (((1,), (0,)), ((), ())), preferred_element_type=F32)


def tn(a, b):
    return lax.dot_general(a, b, (((0,), (0,)), ((), ())), preferred_element_type=F32)


def swap(x, axis=0):
    shape = x.shape
    rest = shape[axis] // SIDE**3
    x = x.reshape(shape[:axis] + (SIDE, SIDE, SIDE, rest) + shape[axis + 1 :])
    return jnp.swapaxes(x, axis, axis + 2).reshape(shape)


def exchange(x, blocks):
    out = lax.all_to_all(
        x.reshape(blocks, x.shape[0] // blocks, x.shape[1]), TO, split_axis=0, concat_axis=0, tiled=True
    )
    return out.reshape(x.shape)


def shift(x, axis, step):
    return lax.ppermute(x, axis, [(i, (i + step) % SIDE) for i in range(SIDE)])


def gate(m_ref, x_ref):
    x = x_ref[...].astype(F32)
    return (m_ref[...].astype(F32) * (x * jax.nn.sigmoid(x))).astype(BF16)


def grads_kernel(m_ref, x_ref, c_ref, own_ref, other_ref, two_ref, grad_ref, gated, total):
    half = pl.program_id(1)

    @pl.when(half == 0)
    def _():
        gated[...] = gate(m_ref, x_ref)
        total[...] = c_ref[...].astype(F32)

    def add(w_ref):
        up, down = w_ref[0, 0], w_ref[1, 0]
        pre = nt(gated[...], up)
        back = nt(c_ref[...], down)
        square = pre * pre
        t = jnp.tanh(pre * (C0 + (C0 * C1) * square))
        slope = 0.5 + 0.5 * t + (0.5 * pre) * (1.0 - t * t) * (C0 + (3.0 * C0 * C1) * square)
        total[...] += nn((back * slope).astype(BF16), up)

    @pl.when(half == 0)
    def _():
        add(own_ref)

    @pl.when(half == 1)
    def _():
        add(other_ref)
        x = x_ref[...].astype(F32)
        grad_ref[...] = total[...]
        two_ref[...] = (total[...] * (x * jax.nn.sigmoid(x))).astype(BF16)


def outputs_kernel(rows, m_ref, x_ref, own_ref, other_ref, out_ref, gated, total):
    half = pl.program_id(1)

    @pl.when(half == 0)
    def _():
        gated[...] = gate(m_ref, x_ref)
        total[...] = gated[...].astype(F32)

    def add(w_ref):
        up, down = w_ref[0, 0], w_ref[1, 0]
        for at in range(0, gated.shape[0], rows):
            part = pl.ds(at, rows)
            pre = nt(gated[part, :], up)
            t = jnp.tanh(pre * (C0 + (C0 * C1) * (pre * pre)))
            total[part, :] += nn((pre * (0.5 + 0.5 * t)).astype(BF16), down)

    @pl.when(half == 0)
    def _():
        add(own_ref)

    @pl.when(half == 1)
    def _():
        add(other_ref)
        out_ref[...] = total[...].astype(BF16)


def mlp_call(kernel, arrays, weights, out_types, dots):
    tokens, channels = arrays[0].shape
    _, groups, hid, group_ch = weights[0].shape
    cols = pl.BlockSpec((tokens, group_ch), lambda g, h: (0, g))
    whole = pl.BlockSpec((2, 1, hid, group_ch), lambda g, h: (0, g, 0, 0))
    units = len(weights) * hid
    return pl.pallas_call(
        kernel,
        grid=(groups, len(weights)),
        in_specs=[cols] * len(arrays) + [whole] * len(weights),
        out_specs=[cols] * len(out_types),
        out_shape=[jax.ShapeDtypeStruct((tokens, channels), t) for t in out_types],
        scratch_shapes=[pltpu.VMEM((tokens, group_ch), BF16), pltpu.VMEM((tokens, group_ch), F32)],
        cost_estimate=pl.CostEstimate(
            flops=2 * dots * tokens * channels * units,
            transcendentals=tokens * units * groups,
            bytes_accessed=2 * len(arrays) * tokens * channels + 4 * channels * units,
        ),
    )(*arrays, *weights)


def weight_column(up_weight, down_weight):
    slabs = jnp.stack([jnp.swapaxes(up_weight, 1, 2), down_weight])
    slabs = slabs.reshape(slabs.shape[:2] + (WEIGHT_SLICES, -1, slabs.shape[-1]))
    y, x = lax.axis_index("y"), lax.axis_index("x")
    place = (y * 2 + lax.rem(x, 2), x * 2 + lax.rem(y, 2))
    piece = jnp.stack([lax.dynamic_index_in_dim(slabs[i], place[i], axis=1, keepdims=False) for i in (0, 1)])
    column = lax.all_to_all(
        jnp.broadcast_to(piece[None], (SIDE, *piece.shape)), "lo", split_axis=0, concat_axis=0, tiled=True
    )
    return slabs, column


def assemble_kernel(at_ref, slabs_ref, *refs):
    out_ref = refs[-1]
    own = slabs_ref.shape[2]
    out_ref[:, :, :own] = slabs_ref[...]
    for i, pieces in ((0, refs[:SIDE]), (1, refs[SIDE : 2 * SIDE])):
        along, across = at_ref[i], lax.rem(at_ref[1 - i], 2)
        for step, piece_ref in enumerate(pieces):
            source = lax.rem(along + SIDE - step, SIDE)
            twin = source + 1 - 2 * lax.rem(source, 2)
            first, second = own + 3 * (source * 2 + across), own + 3 * (twin * 2 + 1 - across)
            out_ref[i, :, pl.ds(first, 3)] = piece_ref[0]
            out_ref[i, :, pl.ds(second, 3)] = piece_ref[1]


def weight_pairs(column):
    lo = lax.axis_index("lo")
    others = lax.dynamic_slice_in_dim(jnp.concatenate([column, column]), lo + 1, SIDE - 1, axis=0)
    others = jnp.moveaxis(others, 0, 2)
    diagonal = [((y * SIDE + x), ((y ^ 1) * SIDE + (x ^ 1))) for y in range(SIDE) for x in range(SIDE)]
    twin = lax.ppermute(others, ("y", "x"), diagonal)
    return jnp.stack([others, twin], axis=1)


def weight_halves(slabs, pairs):
    ups = [pairs[0]] + [shift(pairs[0], "y", k) for k in (1, 2, 3)]
    downs = [pairs[1]] + [shift(pairs[1], "x", k) for k in (1, 2, 3)]
    at = jnp.stack([lax.axis_index("y"), lax.axis_index("x")]).astype(jnp.int32)
    _, groups, own, rows, group_ch = slabs.shape
    half = pl.pallas_call(
        assemble_kernel,
        in_specs=[pl.BlockSpec(memory_space=pltpu.SMEM)] + [pl.BlockSpec(memory_space=pltpu.VMEM)] * 9,
        out_specs=pl.BlockSpec(memory_space=pltpu.VMEM),
        out_shape=jax.ShapeDtypeStruct((2, groups, 4 * own, rows, group_ch), BF16),
        cost_estimate=pl.CostEstimate(flops=0, transcendentals=0, bytes_accessed=16 * slabs.size),
        name="assemble",
    )(at, slabs, *ups, *downs)
    half = half.reshape(2, groups, 4 * own * rows, group_ch)
    return half, lax.ppermute(half, "core", [(0, 1), (1, 0)])


def mix_kernel(two_ref, x_ref, out_ref):
    out_ref[...] = nn(two_ref[...], x_ref[...]).astype(BF16)


def mix(two, x):
    rows, channels = x.shape
    cols = pl.BlockSpec((rows, channels // 2), lambda i: (0, i))
    return pl.pallas_call(
        mix_kernel,
        grid=(2,),
        in_specs=[pl.BlockSpec(two.shape, lambda i: (0, 0)), cols],
        out_specs=cols,
        out_shape=jax.ShapeDtypeStruct(x.shape, BF16),
        cost_estimate=pl.CostEstimate(
            flops=2 * rows * rows * channels, transcendentals=0, bytes_accessed=4 * rows * channels + 2 * rows * rows
        ),
    )(two, x)


def layer(inputs, cotangent, factor_one, factor_two, up_weight, down_weight):
    block = factor_one.shape[1]
    own_p, blocks, _ = factor_two.shape
    n_dp = SIDE * CORES
    x_nat = inputs[0]

    slabs, column = weight_column(up_weight, down_weight)
    one = swap(factor_one[0])
    mixed_one = nn(one, x_nat).astype(BF16)
    mixed_one, column = lax.optimization_barrier((mixed_one, column))
    cols_one = exchange(mixed_one, blocks)

    at = lax.broadcasted_iota(jnp.int32, (blocks, block), 1) // own_p
    at = lax.rem(at, SIDE) * SIDE**2 + lax.rem(at // SIDE, SIDE) * SIDE + at // SIDE**2
    pick = (at == lax.broadcasted_iota(jnp.int32, (blocks, block), 0)).astype(BF16)

    def diagonal(full):
        row = lax.broadcasted_iota(jnp.int32, (block, block), 0)
        col = lax.broadcasted_iota(jnp.int32, (block, block), 1)
        return jnp.where(lax.rem(row, own_p) == lax.rem(col, own_p), full, 0.0).astype(BF16)

    by_q = swap(jnp.transpose(factor_two, (1, 0, 2))).reshape(block, blocks)
    two = diagonal(nn(by_q, pick))
    two_t = two.T
    pairs = weight_pairs(column)
    x_all, cot_all = swap(x_nat), swap(cotangent[0])
    cols_one, _, two, two_t, x_all, cot_all = lax.optimization_barrier((cols_one, pairs, two, two_t, x_all, cot_all))

    weights = weight_halves(slabs, pairs)
    mixed_two = mix(two, cols_one)
    mixed = exchange(mixed_two, blocks)

    grad_two, grad_gated = mlp_call(grads_kernel, (mixed, x_all, cot_all), weights, (BF16, F32), 3)
    grad_cols = exchange(grad_two, blocks)

    (outputs,) = mlp_call(functools.partial(outputs_kernel, 256), (mixed, x_all), weights, (BF16,), 2)
    outputs = swap(outputs)[None]
    gate_in = swap(jax.vjp(jax.nn.silu, x_all.astype(F32))[1](grad_gated * mixed.astype(F32))[0])
    grad_cols, outputs, gate_in = lax.optimization_barrier((grad_cols, outputs, gate_in))

    grad_one = exchange(mix(two_t, grad_cols), blocks)

    term_two = nt(diagonal(nt(grad_cols, cols_one)), pick).astype(BF16)
    term_two = swap(term_two.reshape(blocks, own_p * blocks)).reshape(n_dp, -1, block)
    grad_one, term_two = lax.optimization_barrier((grad_one, term_two))

    term_one = swap(nt(grad_one, x_nat).astype(BF16)).reshape(n_dp, block // n_dp, block)
    terms = jnp.concatenate([term_one, term_two], axis=1)
    terms = terms.reshape(SIDE, CORES, *terms.shape[1:])
    core = lax.axis_index("core")
    kept = lax.dynamic_index_in_dim(terms, core, axis=1, keepdims=False)
    other = lax.ppermute(lax.dynamic_index_in_dim(terms, 1 - core, axis=1, keepdims=False), "core", [(0, 1), (1, 0)])
    terms = (kept.astype(F32) + other.astype(F32)).astype(BF16)
    terms = lax.all_to_all(terms, "lo", split_axis=0, concat_axis=0, tiled=True)
    chunk = block // n_dp
    grad_first = jnp.sum(terms[:, :chunk].astype(F32), axis=0)[None]
    grad_second = jnp.sum(terms[:, chunk:].astype(F32), axis=0).reshape(blocks // n_dp, own_p, blocks)
    grad_second = jnp.transpose(grad_second, (1, 0, 2))

    grad_inputs = (gate_in + tn(one, grad_one)).astype(BF16)[None]
    return outputs, grad_inputs, grad_first, grad_second


def solution(mesh):
    grid = Mesh(mesh.devices.reshape(SIDE, CORES, SIDE, SIDE, SIDE), ("lo", "core", "y", "hi", "x"))
    dp, seq = ("lo", "core"), ("y", "hi", "x")
    in_specs = (P(dp, seq, None), P(dp, seq, None), P(seq, None, None), P(seq, None, None), P(None, None, dp), P(None, dp, None))
    out_specs = (P(dp, seq, None), P(dp, seq, None), P(seq, dp, None), P(seq, dp, None))
    return jax.shard_map(layer, mesh=grid, in_specs=in_specs, out_specs=out_specs, check_vma=False)
```

```python
import functools

import jax
import jax.numpy as jnp
from jax import lax
from jax.experimental import pallas as pl
from jax.experimental.layout import Layout, with_layout_constraint
from jax.experimental.pallas import tpu as pltpu
from jax.sharding import Mesh
from jax.sharding import PartitionSpec as P


F32 = jnp.float32
BF16 = jnp.bfloat16
SIDE = 4
CORES = 2
CHIPS = SIDE**3
OTHER_WAY = (0, 3, 2, 1)


def exchange_groups():
    return [
        [
            core * CHIPS + (y * SIDE + (OTHER_WAY[hi] if core else hi)) * SIDE + x
            for x in range(SIDE)
            for hi in range(SIDE)
            for y in range(SIDE)
        ]
        for core in range(CORES)
    ]


WEIGHT_SLICES = 8
C0 = 0.7978845608028654
C1 = 0.044715


def nt(a, b):
    return lax.dot_general(a, b, (((1,), (1,)), ((), ())), preferred_element_type=F32)


def nn(a, b):
    return lax.dot_general(a, b, (((1,), (0,)), ((), ())), preferred_element_type=F32)


def tn(a, b):
    return lax.dot_general(a, b, (((0,), (0,)), ((), ())), preferred_element_type=F32)


def row_major(x):
    return with_layout_constraint(x, Layout(major_to_minor=tuple(range(x.ndim))))


def swap(x, axis=0):
    shape = x.shape
    rest = shape[axis] // SIDE**3
    x = x.reshape(shape[:axis] + (SIDE, SIDE, SIDE, rest) + shape[axis + 1 :])
    return jnp.swapaxes(x, axis, axis + 2).reshape(shape)


def exchange(x, blocks):
    out = lax.all_to_all(
        x.reshape(blocks, x.shape[0] // blocks, x.shape[1]),
        ("core", "y", "hi", "x"),
        split_axis=0,
        concat_axis=0,
        tiled=True,
        axis_index_groups=exchange_groups(),
    )
    return out.reshape(x.shape)


def other_way(x):
    parts = x.reshape(SIDE, SIDE, -1, *x.shape[1:])
    turned = jnp.stack([parts[:, hi] for hi in OTHER_WAY], axis=1).reshape(x.shape)
    return jnp.where(lax.axis_index("core") == 1, turned, x)


def turn(x):
    pairs = [(SIDE + hi, SIDE + OTHER_WAY[hi]) for hi in (1, 3)]
    moved = lax.ppermute(x, ("core", "hi"), pairs)
    here = (lax.axis_index("core") == 1) & (lax.rem(lax.axis_index("hi"), 2) == 1)
    return jnp.where(here, moved, x)


def shift(x, axis, step):
    return lax.ppermute(x, axis, [(i, (i + step) % SIDE) for i in range(SIDE)])


def gate(m_ref, x_ref):
    x = x_ref[...].astype(F32)
    return (m_ref[...].astype(F32) * (x * jax.nn.sigmoid(x))).astype(BF16)


def grads_kernel(m_ref, x_ref, c_ref, own_ref, other_ref, two_ref, grad_ref, gated, total):
    half = pl.program_id(1)

    @pl.when(half == 0)
    def _():
        gated[...] = gate(m_ref, x_ref)
        total[...] = c_ref[...].astype(F32)

    def add(w_ref):
        up, down = w_ref[0, 0], w_ref[1, 0]
        pre = nt(gated[...], up)
        back = nt(c_ref[...], down)
        square = pre * pre
        t = jnp.tanh(pre * (C0 + (C0 * C1) * square))
        slope = 0.5 + 0.5 * t + (0.5 * pre) * (1.0 - t * t) * (C0 + (3.0 * C0 * C1) * square)
        total[...] += nn((back * slope).astype(BF16), up)

    @pl.when(half == 0)
    def _():
        add(own_ref)

    @pl.when(half == 1)
    def _():
        add(other_ref)
        x = x_ref[...].astype(F32)
        grad_ref[...] = total[...]
        two_ref[...] = (total[...] * (x * jax.nn.sigmoid(x))).astype(BF16)


def outputs_kernel(rows, m_ref, x_ref, own_ref, other_ref, out_ref, gated, total):
    half = pl.program_id(1)

    @pl.when(half == 0)
    def _():
        gated[...] = gate(m_ref, x_ref)
        total[...] = gated[...].astype(F32)

    def add(w_ref):
        up, down = w_ref[0, 0], w_ref[1, 0]
        for at in range(0, gated.shape[0], rows):
            part = pl.ds(at, rows)
            pre = nt(gated[part, :], up)
            t = jnp.tanh(pre * (C0 + (C0 * C1) * (pre * pre)))
            total[part, :] += nn((pre * (0.5 + 0.5 * t)).astype(BF16), down)

    @pl.when(half == 0)
    def _():
        add(own_ref)

    @pl.when(half == 1)
    def _():
        add(other_ref)
        out_ref[...] = total[...].astype(BF16)


def mlp_call(kernel, arrays, weights, out_types, dots):
    tokens, channels = arrays[0].shape
    _, groups, hid, group_ch = weights[0].shape
    cols = pl.BlockSpec((tokens, group_ch), lambda g, h: (0, g))
    whole = pl.BlockSpec((2, 1, hid, group_ch), lambda g, h: (0, g, 0, 0))
    units = len(weights) * hid
    return pl.pallas_call(
        kernel,
        grid=(groups, len(weights)),
        in_specs=[cols] * len(arrays) + [whole] * len(weights),
        out_specs=[cols] * len(out_types),
        out_shape=[jax.ShapeDtypeStruct((tokens, channels), t) for t in out_types],
        scratch_shapes=[pltpu.VMEM((tokens, group_ch), BF16), pltpu.VMEM((tokens, group_ch), F32)],
        cost_estimate=pl.CostEstimate(
            flops=2 * dots * tokens * channels * units,
            transcendentals=tokens * units * groups,
            bytes_accessed=2 * len(arrays) * tokens * channels + 4 * channels * units,
        ),
    )(*arrays, *weights)


def weight_column(up_weight, down_weight):
    slabs = jnp.stack([jnp.swapaxes(up_weight, 1, 2), down_weight])
    slabs = slabs.reshape(slabs.shape[:2] + (WEIGHT_SLICES, -1, slabs.shape[-1]))
    y, x = lax.axis_index("y"), lax.axis_index("x")
    place = (y * 2 + lax.rem(x, 2), x * 2 + lax.rem(y, 2))
    piece = jnp.stack([lax.dynamic_index_in_dim(slabs[i], place[i], axis=1, keepdims=False) for i in (0, 1)])
    column = lax.all_to_all(
        jnp.broadcast_to(piece[None], (SIDE, *piece.shape)), "lo", split_axis=0, concat_axis=0, tiled=True
    )
    return slabs, column


def assemble_kernel(at_ref, slabs_ref, *refs):
    out_ref = refs[-1]
    own = slabs_ref.shape[2]
    out_ref[:, :, :own] = slabs_ref[...]
    for i, pieces in ((0, refs[:SIDE]), (1, refs[SIDE : 2 * SIDE])):
        along, across = at_ref[i], lax.rem(at_ref[1 - i], 2)
        for step, piece_ref in enumerate(pieces):
            source = lax.rem(along + SIDE - step, SIDE)
            twin = source + 1 - 2 * lax.rem(source, 2)
            first, second = own + 3 * (source * 2 + across), own + 3 * (twin * 2 + 1 - across)
            out_ref[i, :, pl.ds(first, 3)] = piece_ref[0]
            out_ref[i, :, pl.ds(second, 3)] = piece_ref[1]


def weight_pairs(column):
    lo = lax.axis_index("lo")
    others = lax.dynamic_slice_in_dim(jnp.concatenate([column, column]), lo + 1, SIDE - 1, axis=0)
    others = jnp.moveaxis(others, 0, 2)
    diagonal = [((y * SIDE + x), ((y ^ 1) * SIDE + (x ^ 1))) for y in range(SIDE) for x in range(SIDE)]
    twin = lax.ppermute(others, ("y", "x"), diagonal)
    return jnp.stack([others, twin], axis=1)


def weight_halves(slabs, pairs):
    ups = [pairs[0]] + [shift(pairs[0], "y", k) for k in (1, 2, 3)]
    downs = [pairs[1]] + [shift(pairs[1], "x", k) for k in (1, 2, 3)]
    at = jnp.stack([lax.axis_index("y"), lax.axis_index("x")]).astype(jnp.int32)
    _, groups, own, rows, group_ch = slabs.shape
    half = pl.pallas_call(
        assemble_kernel,
        in_specs=[pl.BlockSpec(memory_space=pltpu.SMEM)] + [pl.BlockSpec(memory_space=pltpu.VMEM)] * 9,
        out_specs=pl.BlockSpec(memory_space=pltpu.VMEM),
        out_shape=jax.ShapeDtypeStruct((2, groups, 4 * own, rows, group_ch), BF16),
        cost_estimate=pl.CostEstimate(flops=0, transcendentals=0, bytes_accessed=16 * slabs.size),
        name="assemble",
    )(at, slabs, *ups, *downs)
    half = half.reshape(2, groups, 4 * own * rows, group_ch)
    return half, lax.ppermute(half, "core", [(0, 1), (1, 0)])


def layer(inputs, cotangent, factor_one, factor_two, up_weight, down_weight):
    block = factor_one.shape[1]
    own_p, blocks, _ = factor_two.shape
    n_dp = SIDE * CORES
    x_nat = inputs[0]

    slabs, column = weight_column(up_weight, down_weight)
    one = swap(factor_one[0])
    mixed_one = nn(one, x_nat).astype(BF16)
    mixed_one, column = lax.optimization_barrier((mixed_one, column))
    cols_one = exchange(mixed_one, blocks)

    at = lax.broadcasted_iota(jnp.int32, (blocks, block), 1) // own_p
    hi = lax.rem(at // SIDE, SIDE)
    hi = jnp.where(lax.axis_index("core") == 1, lax.rem(SIDE - hi, SIDE), hi)
    at = lax.rem(at, SIDE) * SIDE**2 + hi * SIDE + at // SIDE**2
    pick = (at == lax.broadcasted_iota(jnp.int32, (blocks, block), 0)).astype(BF16)

    def diagonal(full):
        row = lax.broadcasted_iota(jnp.int32, (block, block), 0)
        col = lax.broadcasted_iota(jnp.int32, (block, block), 1)
        return jnp.where(lax.rem(row, own_p) == lax.rem(col, own_p), full, 0.0).astype(BF16)

    by_q = other_way(swap(jnp.transpose(turn(factor_two), (1, 0, 2)))).reshape(block, blocks)
    two = row_major(diagonal(nn(by_q, pick)))
    two_t = row_major(two.T)
    pairs = weight_pairs(column)
    x_all, cot_all = swap(x_nat), swap(cotangent[0])
    cols_one, _, two, two_t, x_all, cot_all = lax.optimization_barrier((cols_one, pairs, two, two_t, x_all, cot_all))

    weights = weight_halves(slabs, pairs)
    mixed_two = nn(two, cols_one).astype(BF16)
    mixed = exchange(mixed_two, blocks)

    grad_two, grad_gated = mlp_call(grads_kernel, (mixed, x_all, cot_all), weights, (BF16, F32), 3)
    grad_cols = exchange(grad_two, blocks)

    (outputs,) = mlp_call(functools.partial(outputs_kernel, 256), (mixed, x_all), weights, (BF16,), 2)
    outputs = swap(outputs)[None]
    gate_in = swap(jax.vjp(jax.nn.silu, x_all.astype(F32))[1](grad_gated * mixed.astype(F32))[0])
    grad_cols, outputs, gate_in = lax.optimization_barrier((grad_cols, outputs, gate_in))

    grad_one = exchange(nn(two_t, grad_cols).astype(BF16), blocks)

    term_two = nt(diagonal(nt(grad_cols, cols_one)), pick).astype(BF16)
    term_two = swap(other_way(term_two.reshape(blocks, own_p * blocks))).reshape(n_dp, -1, block)
    term_two = turn(term_two)
    grad_one, term_two = lax.optimization_barrier((grad_one, term_two))

    term_one = swap(nt(grad_one, x_nat).astype(BF16)).reshape(n_dp, block // n_dp, block)
    terms = jnp.concatenate([term_one, term_two], axis=1)
    terms = terms.reshape(SIDE, CORES, *terms.shape[1:])
    core = lax.axis_index("core")
    kept = lax.dynamic_index_in_dim(terms, core, axis=1, keepdims=False)
    other = lax.ppermute(lax.dynamic_index_in_dim(terms, 1 - core, axis=1, keepdims=False), "core", [(0, 1), (1, 0)])
    terms = (kept.astype(F32) + other.astype(F32)).astype(BF16)
    terms = lax.all_to_all(terms, "lo", split_axis=0, concat_axis=0, tiled=True)
    chunk = block // n_dp
    grad_first = jnp.sum(terms[:, :chunk].astype(F32), axis=0)[None]
    grad_second = jnp.sum(terms[:, chunk:].astype(F32), axis=0).reshape(blocks // n_dp, own_p, blocks)
    grad_second = jnp.transpose(grad_second, (1, 0, 2))

    grad_inputs = (gate_in + tn(one, grad_one)).astype(BF16)[None]
    return outputs, grad_inputs, grad_first, grad_second


def solution(mesh):
    grid = Mesh(mesh.devices.reshape(SIDE, CORES, SIDE, SIDE, SIDE), ("lo", "core", "y", "hi", "x"))
    dp, seq = ("lo", "core"), ("y", "hi", "x")
    in_specs = (P(dp, seq, None), P(dp, seq, None), P(seq, None, None), P(seq, None, None), P(None, None, dp), P(None, dp, None))
    out_specs = (P(dp, seq, None), P(dp, seq, None), P(seq, dp, None), P(seq, dp, None))
    return jax.shard_map(layer, mesh=grid, in_specs=in_specs, out_specs=out_specs, check_vma=False)
```

```python
import functools

import jax
import jax.numpy as jnp
from jax import lax
from jax.experimental import pallas as pl
from jax.experimental.layout import Layout, with_layout_constraint
from jax.experimental.pallas import tpu as pltpu
from jax.sharding import Mesh
from jax.sharding import PartitionSpec as P


F32 = jnp.float32
BF16 = jnp.bfloat16
SIDE = 4
CORES = 2
RING = SIDE * SIDE
TO = ("x", "hi", "y")
WEIGHT_SLICES = 8
C0 = 0.7978845608028654
C1 = 0.044715


def nt(a, b):
    return lax.dot_general(a, b, (((1,), (1,)), ((), ())), preferred_element_type=F32)


def nn(a, b):
    return lax.dot_general(a, b, (((1,), (0,)), ((), ())), preferred_element_type=F32)


def tn(a, b):
    return lax.dot_general(a, b, (((0,), (0,)), ((), ())), preferred_element_type=F32)


def row_major(x):
    return with_layout_constraint(x, Layout(major_to_minor=tuple(range(x.ndim))))


def swap(x, axis=0):
    shape = x.shape
    rest = shape[axis] // SIDE**3
    x = x.reshape(shape[:axis] + (SIDE, SIDE, SIDE, rest) + shape[axis + 1 :])
    return jnp.swapaxes(x, axis, axis + 2).reshape(shape)


def exchange(x, blocks):
    out = lax.all_to_all(
        x.reshape(blocks, x.shape[0] // blocks, x.shape[1]), TO, split_axis=0, concat_axis=0, tiled=True
    )
    return out.reshape(x.shape)


def along_z(x, step):
    at = [(z % SIDE) * SIDE + z // SIDE for z in range(RING)]
    return lax.ppermute(x, ("lo", "hi"), [(at[z], at[(z + step) % RING]) for z in range(RING)])


def shift(x, axis, step):
    return lax.ppermute(x, axis, [(i, (i + step) % SIDE) for i in range(SIDE)])


def gate(m_ref, x_ref):
    x = x_ref[...].astype(F32)
    return (m_ref[...].astype(F32) * (x * jax.nn.sigmoid(x))).astype(BF16)


def grads_kernel(m_ref, x_ref, c_ref, own_ref, other_ref, two_ref, grad_ref, gated, total):
    half = pl.program_id(1)

    @pl.when(half == 0)
    def _():
        gated[...] = gate(m_ref, x_ref)
        total[...] = c_ref[...].astype(F32)

    def add(w_ref):
        up, down = w_ref[0, 0], w_ref[1, 0]
        pre = nt(gated[...], up)
        back = nt(c_ref[...], down)
        square = pre * pre
        t = jnp.tanh(pre * (C0 + (C0 * C1) * square))
        slope = 0.5 + 0.5 * t + (0.5 * pre) * (1.0 - t * t) * (C0 + (3.0 * C0 * C1) * square)
        total[...] += nn((back * slope).astype(BF16), up)

    @pl.when(half == 0)
    def _():
        add(own_ref)

    @pl.when(half == 1)
    def _():
        add(other_ref)
        x = x_ref[...].astype(F32)
        grad_ref[...] = total[...]
        two_ref[...] = (total[...] * (x * jax.nn.sigmoid(x))).astype(BF16)


def outputs_kernel(rows, m_ref, x_ref, own_ref, other_ref, out_ref, gated, total):
    half = pl.program_id(1)

    @pl.when(half == 0)
    def _():
        gated[...] = gate(m_ref, x_ref)
        total[...] = gated[...].astype(F32)

    def add(w_ref):
        up, down = w_ref[0, 0], w_ref[1, 0]
        for at in range(0, gated.shape[0], rows):
            part = pl.ds(at, rows)
            pre = nt(gated[part, :], up)
            t = jnp.tanh(pre * (C0 + (C0 * C1) * (pre * pre)))
            total[part, :] += nn((pre * (0.5 + 0.5 * t)).astype(BF16), down)

    @pl.when(half == 0)
    def _():
        add(own_ref)

    @pl.when(half == 1)
    def _():
        add(other_ref)
        out_ref[...] = total[...].astype(BF16)


def mlp_call(kernel, arrays, weights, out_types, dots):
    tokens, channels = arrays[0].shape
    _, groups, hid, group_ch = weights[0].shape
    cols = pl.BlockSpec((tokens, group_ch), lambda g, h: (0, g))
    whole = pl.BlockSpec((2, 1, hid, group_ch), lambda g, h: (0, g, 0, 0))
    units = len(weights) * hid
    return pl.pallas_call(
        kernel,
        grid=(groups, len(weights)),
        in_specs=[cols] * len(arrays) + [whole] * len(weights),
        out_specs=[cols] * len(out_types),
        out_shape=[jax.ShapeDtypeStruct((tokens, channels), t) for t in out_types],
        scratch_shapes=[pltpu.VMEM((tokens, group_ch), BF16), pltpu.VMEM((tokens, group_ch), F32)],
        cost_estimate=pl.CostEstimate(
            flops=2 * dots * tokens * channels * units,
            transcendentals=tokens * units * groups,
            bytes_accessed=2 * len(arrays) * tokens * channels + 4 * channels * units,
        ),
    )(*arrays, *weights)


def weight_column(up_weight, down_weight):
    slabs = jnp.stack([jnp.swapaxes(up_weight, 1, 2), down_weight])
    slabs = slabs.reshape(slabs.shape[:2] + (WEIGHT_SLICES, -1, slabs.shape[-1]))
    y, x = lax.axis_index("y"), lax.axis_index("x")
    place = (y * 2 + lax.rem(x, 2), x * 2 + lax.rem(y, 2))
    piece = jnp.stack([lax.dynamic_index_in_dim(slabs[i], place[i], axis=1, keepdims=False) for i in (0, 1)])
    column = jnp.stack([along_z(piece, step) for step in (1, -1, 2)], axis=2)
    return slabs, column


def assemble_kernel(at_ref, slabs_ref, *refs):
    out_ref = refs[-1]
    own = slabs_ref.shape[2]
    out_ref[:, :, :own] = slabs_ref[...]
    for i, pieces in ((0, refs[:SIDE]), (1, refs[SIDE : 2 * SIDE])):
        along, across = at_ref[i], lax.rem(at_ref[1 - i], 2)
        for step, piece_ref in enumerate(pieces):
            source = lax.rem(along + SIDE - step, SIDE)
            twin = source + 1 - 2 * lax.rem(source, 2)
            first, second = own + 3 * (source * 2 + across), own + 3 * (twin * 2 + 1 - across)
            out_ref[i, :, pl.ds(first, 3)] = piece_ref[0]
            out_ref[i, :, pl.ds(second, 3)] = piece_ref[1]


def weight_pairs(others):
    diagonal = [((y * SIDE + x), ((y ^ 1) * SIDE + (x ^ 1))) for y in range(SIDE) for x in range(SIDE)]
    twin = lax.ppermute(others, ("y", "x"), diagonal)
    return jnp.stack([others, twin], axis=1)


def weight_halves(slabs, pairs):
    ups = [pairs[0]] + [shift(pairs[0], "y", k) for k in (1, 2, 3)]
    downs = [pairs[1]] + [shift(pairs[1], "x", k) for k in (1, 2, 3)]
    at = jnp.stack([lax.axis_index("y"), lax.axis_index("x")]).astype(jnp.int32)
    _, groups, own, rows, group_ch = slabs.shape
    half = pl.pallas_call(
        assemble_kernel,
        in_specs=[pl.BlockSpec(memory_space=pltpu.SMEM)] + [pl.BlockSpec(memory_space=pltpu.VMEM)] * 9,
        out_specs=pl.BlockSpec(memory_space=pltpu.VMEM),
        out_shape=jax.ShapeDtypeStruct((2, groups, 4 * own, rows, group_ch), BF16),
        cost_estimate=pl.CostEstimate(flops=0, transcendentals=0, bytes_accessed=16 * slabs.size),
        name="assemble",
    )(at, slabs, *ups, *downs)
    half = half.reshape(2, groups, 4 * own * rows, group_ch)
    return half, lax.ppermute(half, "core", [(0, 1), (1, 0)])


def layer(inputs, cotangent, factor_one, factor_two, up_weight, down_weight):
    block = factor_one.shape[1]
    own_p, blocks, _ = factor_two.shape
    n_dp = SIDE * CORES
    x_nat = inputs[0]

    one = swap(factor_one[0])
    mixed_one = nn(one, x_nat).astype(BF16)
    cols_one = exchange(mixed_one, blocks)
    slabs, column = weight_column(up_weight, down_weight)

    at = lax.broadcasted_iota(jnp.int32, (blocks, block), 1) // own_p
    at = lax.rem(at, SIDE) * SIDE**2 + lax.rem(at // SIDE, SIDE) * SIDE + at // SIDE**2
    pick = (at == lax.broadcasted_iota(jnp.int32, (blocks, block), 0)).astype(BF16)

    def diagonal(full):
        row = lax.broadcasted_iota(jnp.int32, (block, block), 0)
        col = lax.broadcasted_iota(jnp.int32, (block, block), 1)
        return jnp.where(lax.rem(row, own_p) == lax.rem(col, own_p), full, 0.0).astype(BF16)

    by_q = swap(jnp.transpose(factor_two, (1, 0, 2))).reshape(block, blocks)
    two = row_major(diagonal(nn(by_q, pick)))
    x_all, cot_all = swap(x_nat), swap(cotangent[0])
    cols_one, two, x_all, cot_all = lax.optimization_barrier((cols_one, two, x_all, cot_all))

    weights = weight_halves(slabs, weight_pairs(column))
    mixed_two = nn(two, cols_one).astype(BF16)
    mixed = exchange(mixed_two, blocks)

    grad_two, grad_gated = mlp_call(grads_kernel, (mixed, x_all, cot_all), weights, (BF16, F32), 3)
    grad_cols = exchange(grad_two, blocks)

    (outputs,) = mlp_call(functools.partial(outputs_kernel, 256), (mixed, x_all), weights, (BF16,), 2)
    outputs = swap(outputs)[None]
    gate_in = swap(jax.vjp(jax.nn.silu, x_all.astype(F32))[1](grad_gated * mixed.astype(F32))[0])
    grad_cols, outputs, gate_in = lax.optimization_barrier((grad_cols, outputs, gate_in))

    grad_one = exchange(tn(two, grad_cols).astype(BF16), blocks)

    term_two = nt(diagonal(nt(grad_cols, cols_one)), pick).astype(BF16)
    term_two = swap(term_two.reshape(blocks, own_p * blocks)).reshape(n_dp, -1, block)
    grad_one, term_two = lax.optimization_barrier((grad_one, term_two))

    term_one = swap(nt(grad_one, x_nat).astype(BF16)).reshape(n_dp, block // n_dp, block)
    terms = jnp.concatenate([term_one, term_two], axis=1)
    terms = terms.reshape(SIDE, CORES, *terms.shape[1:])
    core = lax.axis_index("core")
    kept = lax.dynamic_index_in_dim(terms, core, axis=1, keepdims=False)
    other = lax.ppermute(lax.dynamic_index_in_dim(terms, 1 - core, axis=1, keepdims=False), "core", [(0, 1), (1, 0)])
    terms = (kept.astype(F32) + other.astype(F32)).astype(BF16)
    terms = lax.all_to_all(terms, "lo", split_axis=0, concat_axis=0, tiled=True)
    chunk = block // n_dp
    grad_first = jnp.sum(terms[:, :chunk].astype(F32), axis=0)[None]
    grad_second = jnp.sum(terms[:, chunk:].astype(F32), axis=0).reshape(blocks // n_dp, own_p, blocks)
    grad_second = jnp.transpose(grad_second, (1, 0, 2))

    grad_inputs = (gate_in + tn(one, grad_one)).astype(BF16)[None]
    return outputs, grad_inputs, grad_first, grad_second


def solution(mesh):
    grid = Mesh(mesh.devices.reshape(SIDE, CORES, SIDE, SIDE, SIDE), ("lo", "core", "y", "hi", "x"))
    dp, seq = ("lo", "core"), ("y", "hi", "x")
    in_specs = (P(dp, seq, None), P(dp, seq, None), P(seq, None, None), P(seq, None, None), P(None, None, dp), P(None, dp, None))
    out_specs = (P(dp, seq, None), P(dp, seq, None), P(seq, dp, None), P(seq, dp, None))
    return jax.shard_map(layer, mesh=grid, in_specs=in_specs, out_specs=out_specs, check_vma=False)
```

```python
import functools

import jax
import jax.numpy as jnp
from jax import lax
from jax.experimental import pallas as pl
from jax.experimental.layout import Layout, with_layout_constraint
from jax.experimental.pallas import tpu as pltpu
from jax.sharding import Mesh
from jax.sharding import PartitionSpec as P


F32 = jnp.float32
BF16 = jnp.bfloat16
SIDE = 4
CORES = 2
TO = ("x", "hi", "y")
WEIGHT_SLICES = 8
C0 = 0.7978845608028654
C1 = 0.044715


def nt(a, b):
    return lax.dot_general(a, b, (((1,), (1,)), ((), ())), preferred_element_type=F32)


def nn(a, b):
    return lax.dot_general(a, b, (((1,), (0,)), ((), ())), preferred_element_type=F32)


def tn(a, b):
    return lax.dot_general(a, b, (((0,), (0,)), ((), ())), preferred_element_type=F32)


def row_major(x):
    return with_layout_constraint(x, Layout(major_to_minor=tuple(range(x.ndim))))


def swap(x, axis=0):
    shape = x.shape
    rest = shape[axis] // SIDE**3
    x = x.reshape(shape[:axis] + (SIDE, SIDE, SIDE, rest) + shape[axis + 1 :])
    return jnp.swapaxes(x, axis, axis + 2).reshape(shape)


def exchange(x, blocks):
    out = lax.all_to_all(
        x.reshape(blocks, x.shape[0] // blocks, x.shape[1]), TO, split_axis=0, concat_axis=0, tiled=True
    )
    return out.reshape(x.shape)


def shift(x, axis, step):
    return lax.ppermute(x, axis, [(i, (i + step) % SIDE) for i in range(SIDE)])


def gate(m_ref, x_ref):
    x = x_ref[...].astype(F32)
    return (m_ref[...].astype(F32) * (x * jax.nn.sigmoid(x))).astype(BF16)


def grads_kernel(m_ref, x_ref, c_ref, own_ref, other_ref, two_ref, grad_ref, gated, total):
    half = pl.program_id(1)

    @pl.when(half == 0)
    def _():
        gated[...] = gate(m_ref, x_ref)
        total[...] = c_ref[...].astype(F32)

    def add(w_ref):
        up, down = w_ref[0, 0], w_ref[1, 0]
        pre = nt(gated[...], up)
        back = nt(c_ref[...], down)
        square = pre * pre
        t = jnp.tanh(pre * (C0 + (C0 * C1) * square))
        slope = 0.5 + 0.5 * t + (0.5 * pre) * (1.0 - t * t) * (C0 + (3.0 * C0 * C1) * square)
        total[...] += nn((back * slope).astype(BF16), up)

    @pl.when(half == 0)
    def _():
        add(own_ref)

    @pl.when(half == 1)
    def _():
        add(other_ref)
        x = x_ref[...].astype(F32)
        grad_ref[...] = total[...]
        two_ref[...] = (total[...] * (x * jax.nn.sigmoid(x))).astype(BF16)


def outputs_kernel(rows, m_ref, x_ref, own_ref, other_ref, out_ref, gated, total):
    half = pl.program_id(1)

    @pl.when(half == 0)
    def _():
        gated[...] = gate(m_ref, x_ref)
        total[...] = gated[...].astype(F32)

    def add(w_ref):
        up, down = w_ref[0, 0], w_ref[1, 0]
        for at in range(0, gated.shape[0], rows):
            part = pl.ds(at, rows)
            pre = nt(gated[part, :], up)
            t = jnp.tanh(pre * (C0 + (C0 * C1) * (pre * pre)))
            total[part, :] += nn((pre * (0.5 + 0.5 * t)).astype(BF16), down)

    @pl.when(half == 0)
    def _():
        add(own_ref)

    @pl.when(half == 1)
    def _():
        add(other_ref)
        out_ref[...] = total[...].astype(BF16)


def mlp_call(kernel, arrays, weights, out_types, dots):
    tokens, channels = arrays[0].shape
    _, groups, hid, group_ch = weights[0].shape
    cols = pl.BlockSpec((tokens, group_ch), lambda g, h: (0, g))
    whole = pl.BlockSpec((2, 1, hid, group_ch), lambda g, h: (0, g, 0, 0))
    units = len(weights) * hid
    return pl.pallas_call(
        kernel,
        grid=(groups, len(weights)),
        in_specs=[cols] * len(arrays) + [whole] * len(weights),
        out_specs=[cols] * len(out_types),
        out_shape=[jax.ShapeDtypeStruct((tokens, channels), t) for t in out_types],
        scratch_shapes=[pltpu.VMEM((tokens, group_ch), BF16), pltpu.VMEM((tokens, group_ch), F32)],
        cost_estimate=pl.CostEstimate(
            flops=2 * dots * tokens * channels * units,
            transcendentals=tokens * units * groups,
            bytes_accessed=2 * len(arrays) * tokens * channels + 4 * channels * units,
        ),
    )(*arrays, *weights)


def weight_column(up_weight, down_weight):
    slabs = jnp.stack([jnp.swapaxes(up_weight, 1, 2), down_weight])
    slabs = slabs.reshape(slabs.shape[:2] + (WEIGHT_SLICES, -1, slabs.shape[-1]))
    y, x = lax.axis_index("y"), lax.axis_index("x")
    place = (y * 2 + lax.rem(x, 2), x * 2 + lax.rem(y, 2))
    piece = jnp.stack([lax.dynamic_index_in_dim(slabs[i], place[i], axis=1, keepdims=False) for i in (0, 1)])
    column = lax.all_to_all(
        jnp.broadcast_to(piece[None], (SIDE, *piece.shape)), "lo", split_axis=0, concat_axis=0, tiled=True
    )
    return slabs, column


def assemble_kernel(at_ref, slabs_ref, *refs):
    out_ref = refs[-1]
    own = slabs_ref.shape[2]
    out_ref[:, :, :own] = slabs_ref[...]
    for i, pieces in ((0, refs[:SIDE]), (1, refs[SIDE : 2 * SIDE])):
        along, across = at_ref[i], lax.rem(at_ref[1 - i], 2)
        for step, piece_ref in enumerate(pieces):
            source = lax.rem(along + SIDE - step, SIDE)
            twin = source + 1 - 2 * lax.rem(source, 2)
            first, second = own + 3 * (source * 2 + across), own + 3 * (twin * 2 + 1 - across)
            out_ref[i, :, pl.ds(first, 3)] = piece_ref[0]
            out_ref[i, :, pl.ds(second, 3)] = piece_ref[1]


def weight_pairs(column):
    lo = lax.axis_index("lo")
    others = lax.dynamic_slice_in_dim(jnp.concatenate([column, column]), lo + 1, SIDE - 1, axis=0)
    others = jnp.moveaxis(others, 0, 2)
    diagonal = [((y * SIDE + x), ((y ^ 1) * SIDE + (x ^ 1))) for y in range(SIDE) for x in range(SIDE)]
    twin = lax.ppermute(others, ("y", "x"), diagonal)
    return jnp.stack([others, twin], axis=1)


def weight_halves(slabs, pairs):
    ups = [pairs[0]] + [shift(pairs[0], "y", k) for k in (1, 2, 3)]
    downs = [pairs[1]] + [shift(pairs[1], "x", k) for k in (1, 2, 3)]
    at = jnp.stack([lax.axis_index("y"), lax.axis_index("x")]).astype(jnp.int32)
    _, groups, own, rows, group_ch = slabs.shape
    half = pl.pallas_call(
        assemble_kernel,
        in_specs=[pl.BlockSpec(memory_space=pltpu.SMEM)] + [pl.BlockSpec(memory_space=pltpu.VMEM)] * 9,
        out_specs=pl.BlockSpec(memory_space=pltpu.VMEM),
        out_shape=jax.ShapeDtypeStruct((2, groups, 4 * own, rows, group_ch), BF16),
        cost_estimate=pl.CostEstimate(flops=0, transcendentals=0, bytes_accessed=16 * slabs.size),
        name="assemble",
    )(at, slabs, *ups, *downs)
    half = half.reshape(2, groups, 4 * own * rows, group_ch)
    return half, lax.ppermute(half, "core", [(0, 1), (1, 0)])


def layer(inputs, cotangent, factor_one, factor_two, up_weight, down_weight):
    block = factor_one.shape[1]
    own_p, blocks, _ = factor_two.shape
    n_dp = SIDE * CORES
    x_nat = inputs[0]

    slabs, column = weight_column(up_weight, down_weight)
    one = swap(factor_one[0])
    mixed_one = nn(one, x_nat).astype(BF16)
    mixed_one, column = lax.optimization_barrier((mixed_one, column))
    cols_one = exchange(mixed_one, blocks)

    at = lax.broadcasted_iota(jnp.int32, (blocks, block), 1) // own_p
    at = lax.rem(at, SIDE) * SIDE**2 + lax.rem(at // SIDE, SIDE) * SIDE + at // SIDE**2
    pick = (at == lax.broadcasted_iota(jnp.int32, (blocks, block), 0)).astype(BF16)

    def diagonal(full):
        row = lax.broadcasted_iota(jnp.int32, (block, block), 0)
        col = lax.broadcasted_iota(jnp.int32, (block, block), 1)
        return jnp.where(lax.rem(row, own_p) == lax.rem(col, own_p), full, 0.0).astype(BF16)

    by_q = swap(jnp.transpose(factor_two, (1, 0, 2))).reshape(block, blocks)
    two = row_major(diagonal(nn(by_q, pick)))
    pairs = weight_pairs(column)
    x_all, cot_all = swap(x_nat), swap(cotangent[0])
    cols_one, _, two, x_all, cot_all = lax.optimization_barrier((cols_one, pairs, two, x_all, cot_all))

    weights = weight_halves(slabs, pairs)
    mixed_two = nn(two, cols_one).astype(BF16)
    mixed = exchange(mixed_two, blocks)

    grad_two, grad_gated = mlp_call(grads_kernel, (mixed, x_all, cot_all), weights, (BF16, F32), 3)
    grad_cols = exchange(grad_two, blocks)

    (outputs,) = mlp_call(functools.partial(outputs_kernel, 256), (mixed, x_all), weights, (BF16,), 2)
    outputs = swap(outputs)[None]
    gate_in = swap(jax.vjp(jax.nn.silu, x_all.astype(F32))[1](grad_gated * mixed.astype(F32))[0])
    grad_cols, outputs, gate_in = lax.optimization_barrier((grad_cols, outputs, gate_in))

    grad_one = exchange(tn(two, grad_cols).astype(BF16), blocks)

    term_two = nt(diagonal(nt(grad_cols, cols_one)), pick).astype(BF16)
    term_two = swap(term_two.reshape(blocks, own_p * blocks)).reshape(n_dp, -1, block)
    grad_one, term_two = lax.optimization_barrier((grad_one, term_two))

    term_one = swap(nt(grad_one, x_nat).astype(BF16)).reshape(n_dp, block // n_dp, block)
    terms = jnp.concatenate([term_one, term_two], axis=1)
    terms = terms.reshape(SIDE, CORES, *terms.shape[1:])
    core = lax.axis_index("core")
    kept = lax.dynamic_index_in_dim(terms, core, axis=1, keepdims=False)
    other = lax.ppermute(lax.dynamic_index_in_dim(terms, 1 - core, axis=1, keepdims=False), "core", [(0, 1), (1, 0)])
    terms = (kept.astype(F32) + other.astype(F32)).astype(BF16)
    terms = lax.all_to_all(terms, "lo", split_axis=0, concat_axis=0, tiled=True)
    chunk = block // n_dp
    grad_first = jnp.sum(terms[:, :chunk].astype(F32), axis=0)[None]
    grad_second = jnp.sum(terms[:, chunk:].astype(F32), axis=0).reshape(blocks // n_dp, own_p, blocks)
    grad_second = jnp.transpose(grad_second, (1, 0, 2))

    grad_inputs = (gate_in + tn(one, grad_one)).astype(BF16)[None]
    return outputs, grad_inputs, grad_first, grad_second


def solution(mesh):
    grid = Mesh(mesh.devices.reshape(SIDE, CORES, SIDE, SIDE, SIDE), ("lo", "core", "y", "hi", "x"))
    dp, seq = ("lo", "core"), ("y", "hi", "x")
    in_specs = (P(dp, seq, None), P(dp, seq, None), P(seq, None, None), P(seq, None, None), P(None, None, dp), P(None, dp, None))
    out_specs = (P(dp, seq, None), P(dp, seq, None), P(seq, dp, None), P(seq, dp, None))
    return jax.shard_map(layer, mesh=grid, in_specs=in_specs, out_specs=out_specs, check_vma=False)
```

```python
import functools

import jax
import jax.numpy as jnp
from jax import lax
from jax.experimental import pallas as pl
from jax.experimental.pallas import tpu as pltpu
from jax.sharding import Mesh
from jax.sharding import PartitionSpec as P


F32 = jnp.float32
BF16 = jnp.bfloat16
SIDE = 4
CORES = 2
RING = SIDE * SIDE
TO = ("x", "hi", "y")
WEIGHT_SLICES = 8
C0 = 0.7978845608028654
C1 = 0.044715


def nt(a, b):
    return lax.dot_general(a, b, (((1,), (1,)), ((), ())), preferred_element_type=F32)


def nn(a, b):
    return lax.dot_general(a, b, (((1,), (0,)), ((), ())), preferred_element_type=F32)


def tn(a, b):
    return lax.dot_general(a, b, (((0,), (0,)), ((), ())), preferred_element_type=F32)


def swap(x, axis=0):
    shape = x.shape
    rest = shape[axis] // SIDE**3
    x = x.reshape(shape[:axis] + (SIDE, SIDE, SIDE, rest) + shape[axis + 1 :])
    return jnp.swapaxes(x, axis, axis + 2).reshape(shape)


def exchange(x, blocks):
    out = lax.all_to_all(
        x.reshape(blocks, x.shape[0] // blocks, x.shape[1]), TO, split_axis=0, concat_axis=0, tiled=True
    )
    return out.reshape(x.shape)


def along_z(x, step):
    at = [(z % SIDE) * SIDE + z // SIDE for z in range(RING)]
    return lax.ppermute(x, ("lo", "hi"), [(at[z], at[(z + step) % RING]) for z in range(RING)])


def shift(x, axis, step):
    return lax.ppermute(x, axis, [(i, (i + step) % SIDE) for i in range(SIDE)])


def gate(m_ref, x_ref):
    x = x_ref[...].astype(F32)
    return (m_ref[...].astype(F32) * (x * jax.nn.sigmoid(x))).astype(BF16)


def grads_kernel(m_ref, x_ref, c_ref, own_ref, other_ref, two_ref, grad_ref, gated, total):
    half = pl.program_id(1)

    @pl.when(half == 0)
    def _():
        gated[...] = gate(m_ref, x_ref)
        total[...] = c_ref[...].astype(F32)

    def add(w_ref):
        up, down = w_ref[0, 0], w_ref[0, 1]
        pre = nt(gated[...], up)
        back = nt(c_ref[...], down)
        square = pre * pre
        t = jnp.tanh(pre * (C0 + (C0 * C1) * square))
        slope = 0.5 + 0.5 * t + (0.5 * pre) * (1.0 - t * t) * (C0 + (3.0 * C0 * C1) * square)
        total[...] += nn((back * slope).astype(BF16), up)

    @pl.when(half == 0)
    def _():
        add(own_ref)

    @pl.when(half == 1)
    def _():
        add(other_ref)
        x = x_ref[...].astype(F32)
        grad_ref[...] = total[...]
        two_ref[...] = (total[...] * (x * jax.nn.sigmoid(x))).astype(BF16)


def outputs_kernel(rows, m_ref, x_ref, own_ref, other_ref, out_ref, gated, total):
    half = pl.program_id(1)

    @pl.when(half == 0)
    def _():
        gated[...] = gate(m_ref, x_ref)
        total[...] = gated[...].astype(F32)

    def add(w_ref):
        up, down = w_ref[0, 0], w_ref[0, 1]
        for at in range(0, gated.shape[0], rows):
            part = pl.ds(at, rows)
            pre = nt(gated[part, :], up)
            t = jnp.tanh(pre * (C0 + (C0 * C1) * (pre * pre)))
            total[part, :] += nn((pre * (0.5 + 0.5 * t)).astype(BF16), down)

    @pl.when(half == 0)
    def _():
        add(own_ref)

    @pl.when(half == 1)
    def _():
        add(other_ref)
        out_ref[...] = total[...].astype(BF16)


def mlp_call(kernel, arrays, weights, out_types, dots):
    tokens, channels = arrays[0].shape
    groups, _, hid, group_ch = weights[0].shape
    cols = pl.BlockSpec((tokens, group_ch), lambda g, h: (0, g))
    whole = pl.BlockSpec((1, 2, hid, group_ch), lambda g, h: (g, 0, 0, 0))
    units = len(weights) * hid
    return pl.pallas_call(
        kernel,
        grid=(groups, len(weights)),
        in_specs=[cols] * len(arrays) + [whole] * len(weights),
        out_specs=[cols] * len(out_types),
        out_shape=[jax.ShapeDtypeStruct((tokens, channels), t) for t in out_types],
        scratch_shapes=[pltpu.VMEM((tokens, group_ch), BF16), pltpu.VMEM((tokens, group_ch), F32)],
        cost_estimate=pl.CostEstimate(
            flops=2 * dots * tokens * channels * units,
            transcendentals=tokens * units * groups,
            bytes_accessed=2 * len(arrays) * tokens * channels + 4 * channels * units,
        ),
    )(*arrays, *weights)


def weight_column(up_weight, down_weight):
    own_hid = up_weight.shape[2]
    rows = own_hid // WEIGHT_SLICES
    own = jnp.stack([jnp.swapaxes(up_weight, 1, 2), down_weight], axis=1)
    place = lax.axis_index("y") * 2 + lax.rem(lax.axis_index("x"), 2)
    piece = lax.dynamic_slice_in_dim(own, place * rows, rows, axis=2)
    column = [along_z(piece, step) for step in (1, -1, 2)]
    return own, jnp.concatenate(column, axis=2)


def weight_pair(column):
    other = lax.ppermute(column, "x", [(i, i ^ 1) for i in range(SIDE)])
    return jnp.concatenate([column, other], axis=2)


def weight_halves(own, pair):
    others = [shift(pair, "y", k) for k in (1, 2, 3)]
    half = jnp.concatenate([own, pair] + others, axis=2)
    return half, lax.ppermute(half, "core", [(0, 1), (1, 0)])


def layer(inputs, cotangent, factor_one, factor_two, up_weight, down_weight):
    block = factor_one.shape[1]
    own_p, blocks, _ = factor_two.shape
    n_dp = SIDE * CORES
    x_nat = inputs[0]

    own, column = weight_column(up_weight, down_weight)
    one = swap(factor_one[0])
    mixed_one = nn(one, x_nat).astype(BF16)
    mixed_one, column = lax.optimization_barrier((mixed_one, column))
    cols_one = exchange(mixed_one, blocks)

    at = lax.broadcasted_iota(jnp.int32, (blocks, block), 1) // own_p
    at = lax.rem(at, SIDE) * SIDE**2 + lax.rem(at // SIDE, SIDE) * SIDE + at // SIDE**2
    pick = (at == lax.broadcasted_iota(jnp.int32, (blocks, block), 0)).astype(BF16)

    def diagonal(full):
        row = lax.broadcasted_iota(jnp.int32, (block, block), 0)
        col = lax.broadcasted_iota(jnp.int32, (block, block), 1)
        return jnp.where(lax.rem(row, own_p) == lax.rem(col, own_p), full, 0.0).astype(BF16)

    by_q = swap(jnp.transpose(factor_two, (1, 0, 2))).reshape(block, blocks)
    two = diagonal(nn(by_q, pick))
    pair = weight_pair(column)
    x_all, cot_all = swap(x_nat), swap(cotangent[0])
    cols_one, _, two, x_all, cot_all = lax.optimization_barrier((cols_one, pair, two, x_all, cot_all))

    weights = weight_halves(own, pair)
    mixed_two = nn(two, cols_one).astype(BF16)
    mixed = exchange(mixed_two, blocks)

    grad_two, grad_gated = mlp_call(grads_kernel, (mixed, x_all, cot_all), weights, (BF16, F32), 3)
    grad_cols = exchange(grad_two, blocks)

    (outputs,) = mlp_call(functools.partial(outputs_kernel, 256), (mixed, x_all), weights, (BF16,), 2)
    outputs = swap(outputs)[None]
    gate_in = swap(jax.vjp(jax.nn.silu, x_all.astype(F32))[1](grad_gated * mixed.astype(F32))[0])
    grad_cols, outputs, gate_in = lax.optimization_barrier((grad_cols, outputs, gate_in))

    grad_one = exchange(tn(two, grad_cols).astype(BF16), blocks)

    term_two = nt(diagonal(nt(grad_cols, cols_one)), pick).astype(BF16)
    term_two = swap(term_two.reshape(blocks, own_p * blocks)).reshape(n_dp, -1, block)
    grad_one, term_two = lax.optimization_barrier((grad_one, term_two))

    term_one = swap(nt(grad_one, x_nat).astype(BF16)).reshape(n_dp, block // n_dp, block)
    terms = jnp.concatenate([term_one, term_two], axis=1)
    terms = terms.reshape(SIDE, CORES, *terms.shape[1:])
    core = lax.axis_index("core")
    kept = lax.dynamic_index_in_dim(terms, core, axis=1, keepdims=False)
    other = lax.ppermute(lax.dynamic_index_in_dim(terms, 1 - core, axis=1, keepdims=False), "core", [(0, 1), (1, 0)])
    terms = (kept.astype(F32) + other.astype(F32)).astype(BF16)
    terms = lax.all_to_all(terms, "lo", split_axis=0, concat_axis=0, tiled=True)
    chunk = block // n_dp
    grad_first = jnp.sum(terms[:, :chunk].astype(F32), axis=0)[None]
    grad_second = jnp.sum(terms[:, chunk:].astype(F32), axis=0).reshape(blocks // n_dp, own_p, blocks)
    grad_second = jnp.transpose(grad_second, (1, 0, 2))

    grad_inputs = (gate_in + tn(one, grad_one)).astype(BF16)[None]
    return outputs, grad_inputs, grad_first, grad_second


def solution(mesh):
    grid = Mesh(mesh.devices.reshape(SIDE, CORES, SIDE, SIDE, SIDE), ("lo", "core", "y", "hi", "x"))
    dp, seq = ("lo", "core"), ("y", "hi", "x")
    in_specs = (P(dp, seq, None), P(dp, seq, None), P(seq, None, None), P(seq, None, None), P(None, None, dp), P(None, dp, None))
    out_specs = (P(dp, seq, None), P(dp, seq, None), P(seq, dp, None), P(seq, dp, None))
    return jax.shard_map(layer, mesh=grid, in_specs=in_specs, out_specs=out_specs, check_vma=False)
```
